32 devices in a mesh: dp: 8 (over z, x), mp: 4 (over y, core).
Axes of the slice: x: 2, y: 2, z: 4, core: 2. Of those that a mesh axis runs over, the one named last changes fastest.
Arguments:
- inputs: bfloat16 [2, 1024, 2048], P(None, 'dp'), may hold values from -6 to 6
- documents: int32 [2, 1024], P(None, 'dp'), may hold values from 0 to 127, as said below
- cotangent: bfloat16 [2, 1024, 2048], P(None, 'dp'), may hold values from -6 to 6
- qkv_weight: bfloat16 [2, 2048, 3, 2048], P(None, 'dp', None, 'mp'), may hold values from -0.125 to 0.125
- qkv_bias: bfloat16 [2, 3, 8, 256], P(None, None, 'mp', 'dp'), may hold values from -4 to 4
- proj_weight: bfloat16 [2, 2048, 2048], P(None, 'mp', 'dp'), may hold values from -0.375 to 0.375
- proj_bias: bfloat16 [2, 2048], P(None, 'dp'), may hold values from -4 to 4
- expand_weight: bfloat16 [2, 2048, 8192], P(None, 'dp', 'mp'), may hold values from -0.125 to 0.125
- expand_bias: bfloat16 [2, 4, 2048], P(None, 'mp', 'dp'), may hold values from -4 to 4
- shrink_weight: bfloat16 [2, 8192, 2048], P(None, 'mp', 'dp'), may hold values from -0.0625 to 0.0625
- shrink_bias: bfloat16 [2, 2048], P(None, 'dp'), may hold values from -4 to 4
- attn_gain: bfloat16 [2, 2048], P(None, 'dp'), may hold values from 0.5 to 1.5
- attn_shift: bfloat16 [2, 2048], P(None, 'dp'), may hold values from -4 to 4
- mlp_gain: bfloat16 [2, 2048], P(None, 'dp'), may hold values from 0.5 to 1.5
- mlp_shift: bfloat16 [2, 2048], P(None, 'dp'), may hold values from -4 to 4
Outputs:
- outputs: bfloat16 [2, 1024, 2048], P(None, 'dp')
- input_grad: float32 [2, 1024, 2048], P(None, 'dp')
- qkv_weight_grad: float32 [2, 2048, 3, 2048], P(None, 'dp', None, 'mp')
- qkv_bias_grad: float32 [2, 3, 8, 256], P(None, None, 'mp', 'dp')
- proj_weight_grad: float32 [2, 2048, 2048], P(None, 'mp', 'dp')
- proj_bias_grad: float32 [2, 2048], P(None, 'dp')
- expand_weight_grad: float32 [2, 2048, 8192], P(None, 'dp', 'mp')
- expand_bias_grad: float32 [2, 4, 2048], P(None, 'mp', 'dp')
- shrink_weight_grad: float32 [2, 8192, 2048], P(None, 'mp', 'dp')
- shrink_bias_grad: float32 [2, 2048], P(None, 'dp')
- attn_gain_grad: float32 [2, 2048], P(None, 'dp')
- attn_shift_grad: float32 [2, 2048], P(None, 'dp')
- mlp_gain_grad: float32 [2, 2048], P(None, 'dp')
- mlp_shift_grad: float32 [2, 2048], P(None, 'dp')
The draws below stay inside these ranges and needn't reach their ends.
Inputs may be any that keep to these rules, and one draw needn't show every extreme that they name: `documents`: within each aligned block of 128 positions of a micro-batch the numbers start at 0 and rise by 0 or 1 from one position to the next; a run of equal numbers is one document.
All inputs are finite; a program needn't handle non-finite values.
Results may differ from the reference program's by a relative error of at most 0.019.
Values may be sent and summed in bfloat16 or wider, within the bound.
No kernel may reach another device: no remote copies, remote signals or barrier semaphores. Data moves between devices by JAX's collectives and lax.ppermute only.
A program may use at most 320 MiB of HBM per device.

```python
import math
import jax
import jax.numpy as jnp
from jax import lax

D = 2048
FF = 8192
HEADS = 8
HEAD_DIM = 256
ROT = 64
LAYERS = 2
MICRO = 2
TOK_MB = 128
TOKENS = 1024
N_MP = 4


def draw_documents(key, part):
    rate_key, flag_key = jax.random.split(key)
    blocks = TOKENS // TOK_MB
    spacing = jax.random.randint(rate_key, (MICRO, blocks, 1), 3, 300)
    spacing = spacing.at[MICRO - 1, blocks - 1, 0].set(1)
    raw_bits = jax.random.randint(flag_key, (MICRO, blocks, TOK_MB), 0, 1 << 20)
    breaks = (raw_bits % spacing == 0).astype(jnp.int32)
    breaks = breaks.at[:, :, 0].set(1)
    doc_numbers = jnp.cumsum(breaks, axis=-1) - 1
    return doc_numbers.reshape(MICRO, TOKENS).astype(jnp.int32)


def shard_levels(rng, dims, cuts, smallest, top_value):
    def one(dim, blocks):
        draws = jax.random.uniform(jax.random.fold_in(jax.random.fold_in(rng, 6), dim), (blocks,), jnp.float32, smallest / len(cuts), top_value / len(cuts))
        return jnp.repeat(jnp.exp(draws), dims[dim] // blocks).reshape((-1,) + (1,) * (len(dims) - dim - 1))

    factor_of = one(*cuts[0])
    for cut in cuts[1:]:
        factor_of = factor_of * one(*cut)
    return factor_of


def gaussian(stream_key, shape, deviation, limit, cuts=(), kind=jnp.bfloat16):
    level = shard_levels(stream_key, shape, cuts, -0.22, 0.18) if cuts else 1.0
    drawn = jax.random.normal(stream_key, shape, jnp.float32) * deviation * level
    return jnp.minimum(jnp.maximum(drawn, -limit), limit).astype(kind)


def setup_inputs(seed: int = 0) -> dict:
    seeds = jax.random.split(jax.random.key(seed), 16)
    inputs = gaussian(seeds[0], (MICRO, TOKENS, D), 1.0, 6.0, ((1, 8),))
    documents = draw_documents(jax.random.fold_in(seeds[15], 71), 0)
    cotangent = gaussian(seeds[2], (MICRO, TOKENS, D), 1.0, 6.0, ((1, 8),))
    qkv_weight = gaussian(seeds[3], (LAYERS, D, 3, D), D ** -0.5, 0.125, ((1, 8), (3, 4)))
    qkv_bias = gaussian(seeds[4], (LAYERS, 3, HEADS, HEAD_DIM), 0.3, 4.0, ((2, 4), (3, 8)))
    proj_weight = gaussian(seeds[5], (LAYERS, D, D), (D // 8) ** -0.5, 0.375, ((1, 4), (2, 8)))
    proj_bias = gaussian(seeds[6], (LAYERS, D), 0.3, 4.0, ((1, 8),))
    expand_weight = gaussian(seeds[7], (LAYERS, D, FF), D ** -0.5, 0.125, ((1, 8), (2, 4)))
    expand_bias = gaussian(seeds[8], (LAYERS, N_MP, FF // N_MP), 0.3, 4.0, ((1, 4), (2, 8)))
    shrink_weight = gaussian(seeds[9], (LAYERS, FF, D), FF ** -0.5, 0.0625, ((1, 4), (2, 8)))
    shrink_bias = gaussian(seeds[10], (LAYERS, D), 0.3, 4.0, ((1, 8),))
    attn_gain = jnp.clip(1.0 + 0.1 * jax.random.normal(seeds[11], (LAYERS, D), jnp.float32), 0.5, 1.5).astype(jnp.bfloat16)
    attn_shift = gaussian(seeds[12], (LAYERS, D), 0.3, 4.0, ((1, 8),))
    mlp_gain = jnp.clip(1.0 + 0.1 * jax.random.normal(seeds[13], (LAYERS, D), jnp.float32), 0.5, 1.5).astype(jnp.bfloat16)
    mlp_shift = gaussian(seeds[14], (LAYERS, D), 0.3, 4.0, ((1, 8),))
    return {"inputs": inputs, "documents": documents, "cotangent": cotangent, "qkv_weight": qkv_weight, "qkv_bias": qkv_bias, "proj_weight": proj_weight, "proj_bias": proj_bias, "expand_weight": expand_weight, "expand_bias": expand_bias, "shrink_weight": shrink_weight, "shrink_bias": shrink_bias, "attn_gain": attn_gain, "attn_shift": attn_shift, "mlp_gain": mlp_gain, "mlp_shift": mlp_shift}


norm_eps = 1e-05
root_half = 0.7071067811865476
gauss_norm = 0.3989422804014327
masked_score = -1e+30

def contract(form, left, right):
    return jnp.einsum(form, left.astype(jnp.float32), right.astype(jnp.float32))

def matmul(left, right):
    return jnp.dot(left, right, preferred_element_type=jnp.float32)

def doc_tables(doc_numbers):
    row_count = doc_numbers.shape[0]
    across = jnp.arange(row_count, dtype=jnp.int32)
    earlier = jnp.concatenate([doc_numbers[:1] - 1, doc_numbers[:-1]])
    starts = jnp.where(doc_numbers != earlier, across, 0).astype(jnp.int32)
    run_start = lax.cummax(starts, axis=0)
    offset = (across - run_start).astype(jnp.float32)
    allowed = (doc_numbers[:, None] == doc_numbers[None, :]) & (across[None, :] <= across[:, None])
    return (offset, allowed)

def rotary_tables(offset, rotary):
    halfway = rotary // 2
    inverse = jnp.exp(jnp.arange(halfway, dtype=jnp.float32) * (-2.0 * math.log(10000.0) / rotary))
    angles = offset[:, None] * inverse[None, :]
    return (jnp.cos(angles), jnp.sin(angles))

def rotate(head_rows, cosine, sine_table, direction):
    halfway = cosine.shape[1]
    leading = head_rows[..., :halfway]
    trailing = head_rows[..., halfway:2 * halfway]
    cos_rows = cosine[:, None, :]
    sin_rows = sine_table[:, None, :] * direction
    return jnp.concatenate([leading * cos_rows - trailing * sin_rows, trailing * cos_rows + leading * sin_rows, head_rows[..., 2 * halfway:]], axis=-1)

def layer_norm(residual, gain_row, shift_row):
    center = residual - lax.optimization_barrier(jnp.mean(residual, axis=-1, keepdims=True))
    scaled = lax.rsqrt(lax.optimization_barrier(jnp.mean(center * center, axis=-1, keepdims=True)) + norm_eps)
    normed = center * scaled
    return (normed, scaled, normed * gain_row.astype(jnp.float32) + shift_row.astype(jnp.float32))

def norm_back(grad_normed, normed, scaled, gain_row):
    weighted = grad_normed * gain_row.astype(jnp.float32)
    return scaled * (weighted - lax.optimization_barrier(jnp.mean(weighted, axis=-1, keepdims=True)) - normed * lax.optimization_barrier(jnp.mean(weighted * normed, axis=-1, keepdims=True)))

def gelu_exact(preact):
    return 0.5 * preact * (1.0 + lax.erf(preact * root_half))

def gelu_slope(preact):
    return 0.5 * (1.0 + lax.erf(preact * root_half)) + preact * jnp.exp(-0.5 * preact * preact) * gauss_norm

def attend(queries, key_rows, values, allowed):
    factor = queries.shape[-1] ** (-0.5)
    scores = jnp.where(allowed[None], contract('thd,shd->hts', queries, key_rows) * factor, masked_score)
    highest = lax.optimization_barrier(jnp.max(scores, axis=-1, keepdims=True))
    powered = jnp.exp(scores - highest)
    totals = lax.optimization_barrier(jnp.sum(powered, axis=-1, keepdims=True))
    logsum = highest + jnp.log(totals)
    attn_probs = (powered / totals).astype(jnp.bfloat16)
    return (contract('hts,shd->thd', attn_probs, values), logsum)

def attend_back(queries, key_rows, values, allowed, logsum, grad_mixed):
    factor = queries.shape[-1] ** (-0.5)
    scores = jnp.where(allowed[None], contract('thd,shd->hts', queries, key_rows) * factor, masked_score)
    recomputed = jnp.exp(scores - logsum)
    grad_probs = contract('thd,shd->hts', grad_mixed, values)
    inner = lax.optimization_barrier(jnp.sum(recomputed * grad_probs, axis=-1, keepdims=True))
    grad_scores = (recomputed * (grad_probs - inner) * factor).astype(jnp.bfloat16)
    grad_queries = contract('hts,shd->thd', grad_scores, key_rows)
    grad_keys = contract('hts,thd->shd', grad_scores, queries)
    grad_values = contract('hts,thd->shd', recomputed.astype(jnp.bfloat16), grad_mixed)
    return (grad_queries, grad_keys, grad_values)

def forward_parts(residual, cosine, sine_table, allowed, weights):
    qkv_weight, qkv_bias, proj_weight, proj_bias, expand_weight, expand_bias, shrink_weight, shrink_bias, attn_gain, attn_shift, mlp_gain, mlp_shift = weights
    row_count = residual.shape[0]
    model_width = qkv_weight.shape[0]
    local_width = qkv_weight.shape[2]
    heads_here = qkv_bias.shape[1]
    head_width = qkv_bias.shape[2]
    unused_a, unused_b, attn_in = layer_norm(residual, attn_gain, attn_shift)
    unused_c, unused_d, mlp_in = layer_norm(residual, mlp_gain, mlp_shift)
    attn_in = attn_in.astype(jnp.bfloat16)
    mlp_in = mlp_in.astype(jnp.bfloat16)
    projected = matmul(attn_in, qkv_weight.reshape(model_width, 3 * local_width)).reshape(row_count, 3, heads_here, head_width) + qkv_bias.astype(jnp.float32)[None]
    queries = rotate(projected[:, 0], cosine, sine_table, 1.0).astype(jnp.bfloat16)
    key_rows = rotate(projected[:, 1], cosine, sine_table, 1.0).astype(jnp.bfloat16)
    values = projected[:, 2].astype(jnp.bfloat16)
    mixed, logsum = attend(queries, key_rows, values, allowed)
    attn_out = mixed.reshape(row_count, local_width).astype(jnp.bfloat16)
    attn_part = matmul(attn_out, proj_weight)
    preact = matmul(mlp_in, expand_weight) + expand_bias.astype(jnp.float32)
    activated = gelu_exact(preact).astype(jnp.bfloat16)
    mlp_part = matmul(activated, shrink_weight)
    saved = (attn_in, mlp_in, queries, key_rows, values, attn_out, logsum, preact, activated)
    return (attn_part, mlp_part, saved)

def backward_parts(grad_res, saved, weights, cosine, sine_table, allowed):
    qkv_weight, qkv_bias, proj_weight, proj_bias, expand_weight, expand_bias, shrink_weight, shrink_bias, attn_gain, attn_shift, mlp_gain, mlp_shift = weights
    attn_in, mlp_in, queries, key_rows, values, attn_out, logsum, preact, activated = saved
    row_count = grad_res.shape[0]
    model_width = qkv_weight.shape[0]
    local_width = qkv_weight.shape[2]
    heads_here = qkv_bias.shape[1]
    head_width = qkv_bias.shape[2]
    grad_half = grad_res.astype(jnp.bfloat16)
    bias_grad = lax.optimization_barrier(jnp.sum(grad_res, axis=0))
    proj_weight_grad = matmul(attn_out.T, grad_half)
    grad_mixed = matmul(grad_half, proj_weight.T).astype(jnp.bfloat16).reshape(row_count, heads_here, head_width)
    shrink_weight_grad = matmul(activated.T, grad_half)
    grad_preact = matmul(grad_half, shrink_weight.T) * gelu_slope(preact)
    expand_bias_grad = lax.optimization_barrier(jnp.sum(grad_preact, axis=0, keepdims=True))
    grad_pre_half = grad_preact.astype(jnp.bfloat16)
    expand_weight_grad = matmul(mlp_in.T, grad_pre_half)
    grad_mlp_in = matmul(grad_pre_half, expand_weight.T)
    grad_queries, grad_keys, grad_values = attend_back(queries, key_rows, values, allowed, logsum, grad_mixed)
    grad_proj = jnp.stack([rotate(grad_queries, cosine, sine_table, -1.0), rotate(grad_keys, cosine, sine_table, -1.0), grad_values], axis=1)
    qkv_bias_grad = lax.optimization_barrier(jnp.sum(grad_proj, axis=0))
    grad_proj_half = grad_proj.reshape(row_count, 3 * local_width).astype(jnp.bfloat16)
    qkv_weight_grad = matmul(attn_in.T, grad_proj_half).reshape(model_width, 3, local_width)
    grad_attn_in = matmul(grad_proj_half, qkv_weight.reshape(model_width, 3 * local_width).T)
    grads = (qkv_weight_grad, qkv_bias_grad, proj_weight_grad, bias_grad, expand_weight_grad, expand_bias_grad, shrink_weight_grad, bias_grad)
    return (grad_attn_in, grad_mlp_in, grads)

def norm_tail(grad_res, residual, weights, grad_attn_in, grad_mlp_in):
    attn_gain, attn_shift, mlp_gain, mlp_shift = (weights[8], weights[9], weights[10], weights[11])
    normed_attn, scaled_attn, unused_a = layer_norm(residual, attn_gain, attn_shift)
    normed_mlp, scaled_mlp, unused_b = layer_norm(residual, mlp_gain, mlp_shift)
    norm_grads = (lax.optimization_barrier(jnp.sum(grad_attn_in * normed_attn, axis=0)), lax.optimization_barrier(jnp.sum(grad_attn_in, axis=0)), lax.optimization_barrier(jnp.sum(grad_mlp_in * normed_mlp, axis=0)), lax.optimization_barrier(jnp.sum(grad_mlp_in, axis=0)))
    grad_res = grad_res + norm_back(grad_attn_in, normed_attn, scaled_attn, attn_gain) + norm_back(grad_mlp_in, normed_mlp, scaled_mlp, mlp_gain)
    return (grad_res, norm_grads)

def reference(inputs, documents, cotangent, qkv_weight, qkv_bias, proj_weight, proj_bias, expand_weight, expand_bias, shrink_weight, shrink_bias, attn_gain, attn_shift, mlp_gain, mlp_shift):
    blocks = MICRO * (TOKENS // TOK_MB)
    block_rows = inputs.reshape(blocks, TOK_MB, D)
    block_docs = documents.reshape(blocks, TOK_MB)
    block_cots = cotangent.reshape(blocks, TOK_MB, D)
    params = (qkv_weight, qkv_bias, proj_weight, proj_bias, expand_weight, expand_bias, shrink_weight, shrink_bias, attn_gain, attn_shift, mlp_gain, mlp_shift)

    def layer_set(layer_index):
        pieces = [param[layer_index] for param in params]
        pieces[5] = pieces[5].reshape(1, FF)
        return tuple(pieces)
    zeros = tuple((jnp.zeros(param.shape, jnp.float32) for param in params))

    def one_block(carry, block):
        rows_in, docs_in, cots_in = block
        offset, allowed = doc_tables(docs_in)
        cosine, sine_table = rotary_tables(offset, ROT)
        residual = rows_in.astype(jnp.float32)
        kept = []
        for layer_index in range(LAYERS):
            weights = layer_set(layer_index)
            attn_part, mlp_part, saved = forward_parts(residual, cosine, sine_table, allowed, weights)
            kept.append((residual, saved))
            residual = residual + (attn_part + mlp_part) + weights[3].astype(jnp.float32) + weights[7].astype(jnp.float32)
        out_rows = residual.astype(jnp.bfloat16)
        grad_res = cots_in.astype(jnp.float32)
        totals = list(carry)
        for layer_index in reversed(range(LAYERS)):
            weights = layer_set(layer_index)
            layer_input, saved = kept[layer_index]
            grad_attn_in, grad_mlp_in, grads = backward_parts(grad_res, saved, weights, cosine, sine_table, allowed)
            grad_res, norm_grads = norm_tail(grad_res, layer_input, weights, grad_attn_in, grad_mlp_in)
            local_grads = grads + norm_grads
            for index in range(12):
                piece = local_grads[index].reshape(params[index].shape[1:])
                totals[index] = totals[index].at[layer_index].add(piece)
        return (tuple(totals), (out_rows, grad_res))
    totals, (out_blocks, grad_blocks) = lax.scan(one_block, zeros, (block_rows, block_docs, block_cots))
    return (out_blocks.reshape(MICRO, TOKENS, D), grad_blocks.reshape(MICRO, TOKENS, D), totals[0], totals[1], totals[2], totals[3], totals[4], totals[5], totals[6], totals[7], totals[8], totals[9], totals[10], totals[11])
```

```python
import math

import jax
import jax.numpy as jnp
from jax import lax
from jax.sharding import PartitionSpec as P

ROT = 64
norm_eps = 1e-05
root_half = 0.7071067811865476
gauss_norm = 0.3989422804014327
masked_score = -1e30
half = jnp.bfloat16
single = jnp.float32


def dot(left, right, dims):
    return lax.dot_general(left, right, (dims, ((), ())), preferred_element_type=single)


def mm(left, right):
    return dot(left, right, ((1,), (0,)))


def mm_t(left, right):
    return dot(left, right, ((1,), (1,)))


def t_mm(left, right):
    return dot(left, right, ((0,), (0,)))


def swap(values, axis, mask):
    count = lax.axis_size(axis)
    return lax.ppermute(values, axis, [(i, i ^ mask) for i in range(count)])


def pick(values, index, axis):
    return lax.dynamic_index_in_dim(values, index, axis, keepdims=False)


def put(buffer, piece, index, axis):
    return lax.dynamic_update_index_in_dim(buffer, piece, index, axis)


def ordered(bit, mine, other, axis):
    first = bit == 0
    return jnp.stack([jnp.where(first, mine, other), jnp.where(first, other, mine)], axis)


def doc_tables(numbers):
    rows = numbers.shape[0]
    across = jnp.arange(rows, dtype=jnp.int32)
    earlier = jnp.concatenate([numbers[:1] - 1, numbers[:-1]])
    starts = jnp.where(numbers != earlier, across, 0)
    return (across, across - lax.cummax(starts, axis=0))


class Layout:
    def __init__(self, heads_here):
        self.n_dp = lax.axis_size("dp")
        self.n_mp = lax.axis_size("mp")
        self.n_hi = heads_here
        self.n_a = self.n_dp // 2
        self.n_lo = self.n_a // self.n_hi
        self.dp = lax.axis_index("dp")
        self.mp = lax.axis_index("mp")
        self.side = self.dp % 2
        self.a = self.dp // 2
        self.lo = self.a % self.n_lo
        self.hi = self.a // self.n_lo

        def masks(start, count):
            return [start << k for k in range(count.bit_length() - 1)]

        self.lo_masks = masks(2, self.n_lo)
        self.hi_masks = masks(2 * self.n_lo, self.n_hi)
        self.mp_masks = masks(1, self.n_mp)
        steps = [("mp", m) for m in self.mp_masks] + [("dp", m) for m in self.lo_masks]
        self.reduce_steps = steps + [("dp", m) for m in self.hi_masks]

    def gather_rows(self, rows):
        for axis, mask in reversed(self.reduce_steps):
            rows = jnp.concatenate([rows, swap(rows, axis, mask)], 0)
        return rows

    def scatter_rows(self, rows):
        for axis, mask in self.reduce_steps:
            count = rows.shape[0] // 2
            sent = swap(rows[count:].astype(half), axis, mask)
            rows = rows[:count] + sent.astype(single)
        return rows

    def attention_rows(self, rows):
        grouped = rows.reshape((self.n_mp, self.n_lo, -1) + rows.shape[1:])
        return grouped[:, 0].reshape((-1,) + rows.shape[1:])

    def add_attention_rows(self, rows, extra):
        grouped = rows.reshape((self.n_mp, self.n_lo, -1) + rows.shape[1:])
        more = extra.reshape((self.n_mp, 1, -1) + rows.shape[1:])
        if self.n_lo > 1:
            more = jnp.pad(more, ((0, 0), (0, self.n_lo - 1), (0, 0), (0, 0)))
        return (grouped + more).reshape(rows.shape)

    def gather_units(self, pieces):
        buffer = jnp.zeros((self.n_a,) + pieces.shape[1:], pieces.dtype)
        buffer = put(buffer, pick(pieces, self.a, 0), self.a, 0)
        for step in range(1, self.n_a):
            sent = swap(pick(pieces, self.a ^ step, 0), "dp", 2 * step)
            buffer = put(buffer, sent, self.a ^ step, 0)
        return ordered(self.side, buffer, swap(buffer, "dp", 1), 1)

    def scatter_units(self, pieces):
        sent = swap(pick(pieces, 1 - self.side, 1).astype(half), "dp", 1)
        mine = pick(pieces, self.side, 1) + sent.astype(single)
        buffer = jnp.zeros(mine.shape, single)
        buffer = put(buffer, pick(mine, self.a, 0), self.a, 0)
        for step in range(1, self.n_a):
            sent = swap(pick(mine, self.a ^ step, 0).astype(half), "dp", 2 * step)
            buffer = put(buffer, sent.astype(single), self.a ^ step, 0)
        return buffer

    def gather_head(self, pieces):
        buffer = jnp.zeros((self.n_hi,) + pieces.shape[1:], pieces.dtype)
        buffer = put(buffer, pick(pieces, self.hi, 0), self.hi, 0)
        for step in range(1, self.n_hi):
            sent = swap(pick(pieces, self.hi ^ step, 0), "dp", 2 * self.n_lo * step)
            buffer = put(buffer, sent, self.hi ^ step, 0)
        buffer = buffer[:, None]
        for k, mask in enumerate(self.lo_masks):
            both = ordered((self.lo >> k) % 2, buffer, swap(buffer, "dp", mask), 1)
            buffer = both.reshape((self.n_hi, -1) + pieces.shape[1:])
        buffer = ordered(self.side, buffer, swap(buffer, "dp", 1), 2)
        return buffer.reshape((self.n_dp,) + pieces.shape[1:])

    def scatter_head(self, pieces):
        rest = pieces.shape[1:]
        mine = pieces.reshape((self.n_hi, self.n_lo, 2) + rest)
        sent = swap(pick(mine, 1 - self.side, 2).astype(half), "dp", 1)
        mine = pick(mine, self.side, 2) + sent.astype(single)
        for k, mask in reversed(list(enumerate(self.lo_masks))):
            bit = (self.lo >> k) % 2
            mine = mine.reshape((self.n_hi, 2, -1) + rest)
            sent = swap(pick(mine, 1 - bit, 1).astype(half), "dp", mask)
            mine = pick(mine, bit, 1) + sent.astype(single)
        mine = mine.reshape((self.n_hi,) + rest)
        buffer = jnp.zeros(mine.shape, single)
        buffer = put(buffer, pick(mine, self.hi, 0), self.hi, 0)
        for step in range(1, self.n_hi):
            sent = swap(pick(mine, self.hi ^ step, 0).astype(half), "dp", 2 * self.n_lo * step)
            buffer = put(buffer, sent.astype(single), self.hi ^ step, 0)
        return buffer

    def gather_small(self, rows):
        buffer = rows[None]
        for k in range(self.n_dp.bit_length() - 1):
            both = ordered((self.dp >> k) % 2, buffer, swap(buffer, "dp", 1 << k), 0)
            buffer = both.reshape((-1,) + rows.shape)
        return buffer

    def sum_over(self, rows, axis):
        count = lax.axis_size(axis)
        for k in range(count.bit_length() - 1):
            rows = rows + swap(rows, axis, 1 << k)
        return rows


def normalize(residual):
    center = residual - jnp.mean(residual, axis=-1, keepdims=True)
    scaled = lax.rsqrt(jnp.mean(center * center, axis=-1, keepdims=True) + norm_eps)
    return (center * scaled, scaled)


def rotate(rows, cosine, sine):
    halfway = cosine.shape[1]
    leading = rows[:, :halfway]
    trailing = rows[:, halfway : 2 * halfway]
    return jnp.concatenate(
        [leading * cosine - trailing * sine, trailing * cosine + leading * sine, rows[:, 2 * halfway :]],
        axis=-1,
    )


def attend(queries, keys, values, allowed):
    factor = queries.shape[-1] ** (-0.5)
    scores = jnp.where(allowed, mm_t(queries, keys) * factor, masked_score)
    highest = jnp.max(scores, axis=-1, keepdims=True)
    powered = jnp.exp(scores - highest)
    totals = jnp.sum(powered, axis=-1, keepdims=True)
    logsum = highest + jnp.log(totals)
    probs = (powered / totals).astype(half)
    return (mm(probs, values), logsum)


def attend_back(queries, keys, values, allowed, logsum, grad_mixed):
    factor = queries.shape[-1] ** (-0.5)
    scores = jnp.where(allowed, mm_t(queries, keys) * factor, masked_score)
    recomputed = jnp.exp(scores - logsum)
    grad_probs = mm_t(grad_mixed, values)
    inner = jnp.sum(recomputed * grad_probs, axis=-1, keepdims=True)
    grad_scores = (recomputed * (grad_probs - inner) * factor).astype(half)
    return (
        mm(grad_scores, keys),
        t_mm(grad_scores, queries),
        t_mm(recomputed.astype(half), grad_mixed),
    )


def on_device(
    inputs,
    documents,
    cotangent,
    qkv_weight,
    qkv_bias,
    proj_weight,
    proj_bias,
    expand_weight,
    expand_bias,
    shrink_weight,
    shrink_bias,
    attn_gain,
    attn_shift,
    mlp_gain,
    mlp_shift,
):
    depth, shard, _, local_width = qkv_weight.shape
    batches, block, width = inputs.shape
    heads_here, head_shard = qkv_bias.shape[2], qkv_bias.shape[3]
    at = Layout(heads_here)
    head_width = head_shard * at.n_dp
    units = expand_weight.shape[2] // at.n_a
    slice_rows = block // at.n_mp
    chunks = [[m] for m in range(batches)]

    def my_rows(values, chunk):
        cut = [lax.dynamic_slice_in_dim(values[m], at.mp * slice_rows, slice_rows, 0) for m in chunk]
        return jnp.concatenate(cut, 0)

    small = jnp.stack(
        [attn_gain, attn_shift, mlp_gain, mlp_shift, proj_bias, shrink_bias, expand_bias[:, 0]], 1
    ).reshape(depth * 7, shard)
    bias_part = qkv_bias.reshape(-1)
    bias_rows = -(-bias_part.shape[0] // shard)
    bias_part = jnp.pad(bias_part, (0, bias_rows * shard - bias_part.shape[0]))
    small = at.gather_small(jnp.concatenate([small, bias_part.reshape(bias_rows, shard)], 0))
    wide = small[:, : depth * 7].reshape(at.n_dp, depth, 7, shard).transpose(1, 2, 0, 3)
    biases = small[:, depth * 7 :].reshape(at.n_dp, -1)[:, : depth * 3 * heads_here * head_shard]
    biases = biases.reshape(at.n_dp, depth, 3, heads_here, head_shard).transpose(3, 1, 2, 0, 4)
    biases = pick(biases, at.hi, 0).reshape(depth, 3 * head_width).astype(single)
    flat = wide.reshape(depth, 7, width).astype(single)
    unit_bias = pick(wide[:, 6].reshape(depth, at.n_a, units), at.a, 1).astype(single)

    masks = []
    for chunk in chunks:
        cells = []
        for m in chunk:
            place, offset = doc_tables(documents[m])
            cells.append(jnp.stack([documents[m], place, offset], 1).astype(half))
        cells = at.attention_rows(at.gather_rows(my_rows(cells, range(len(chunk))))).astype(single)
        count = cells.shape[0]
        row = lax.iota(jnp.int32, count) // slice_rows % (len(chunk) * at.n_hi)
        inverse = jnp.exp(
            jnp.arange(ROT // 2, dtype=single) * (-2.0 * math.log(10000.0) / ROT)
        )
        angles = cells[:, 2:3] * inverse[None, :]
        flipped = cells.T
        allowed = (
            (row[:, None] == row[None, :])
            & (cells[:, 0:1] == flipped[0:1])
            & (flipped[1:2] <= cells[:, 1:2])
        )
        masks.append((jnp.cos(angles), jnp.sin(angles), allowed))

    def weights_of(layer):
        qkv = qkv_weight[layer].reshape(shard, 3, heads_here, head_width).transpose(2, 0, 1, 3)
        qkv = at.gather_head(qkv.reshape(heads_here, shard, 3 * head_width))
        expand = expand_weight[layer].reshape(shard, at.n_a, units).transpose(1, 0, 2)
        expand = at.gather_units(expand)
        proj = at.gather_head(proj_weight[layer].reshape(heads_here, head_width, shard))
        shrink = at.gather_units(shrink_weight[layer].reshape(at.n_a, units, shard))
        return (
            qkv.reshape(width, 3 * head_width),
            proj.transpose(1, 0, 2).reshape(head_width, width),
            expand.reshape(width, units),
            shrink.transpose(2, 0, 1, 3).reshape(units, width),
        )

    weights = [weights_of(layer) for layer in range(depth)]

    residuals = [my_rows(inputs, chunk).astype(single) for chunk in chunks]
    saved = []
    for layer in range(depth):
        gain_a, shift_a, gain_m, shift_m, bias_p, bias_s = [flat[layer, k] for k in range(6)]
        qkv, proj, expand, shrink = weights[layer]
        kept = []
        for which, chunk in enumerate(chunks):
            cosine, sine, allowed = masks[which]
            normed, scaled = normalize(residuals[which])
            rows = at.gather_rows(normed.astype(half))
            rows_a = at.attention_rows(rows)
            attn_in = (rows_a.astype(single) * gain_a + shift_a).astype(half)
            mlp_in = (rows.astype(single) * gain_m + shift_m).astype(half)
            projected = mm(attn_in, qkv) + biases[layer]
            queries = rotate(projected[:, :head_width], cosine, sine).astype(half)
            keys = rotate(projected[:, head_width : 2 * head_width], cosine, sine).astype(half)
            values = projected[:, 2 * head_width :].astype(half)
            mixed, logsum = attend(queries, keys, values, allowed)
            attn_out = mixed.astype(half)
            preact = mm(mlp_in, expand) + unit_bias[layer]
            activated = (0.5 * preact * (1.0 + lax.erf(preact * root_half))).astype(half)
            parts = at.add_attention_rows(mm(activated, shrink), mm(attn_out, proj))
            residuals[which] = residuals[which] + at.scatter_rows(parts) + bias_p + bias_s
            kept.append(
                (normed, scaled, rows, rows_a, attn_in, mlp_in, queries, keys, values, attn_out, logsum, preact, activated)
            )
        saved.append(kept)

    def whole_rows(parts):
        rows = jnp.stack(parts).reshape(batches, slice_rows, width)
        for k, mask in enumerate(at.mp_masks):
            both = ordered((at.mp >> k) % 2, rows, swap(rows, "mp", mask), 1)
            rows = both.reshape(batches, -1, width)
        return rows

    outputs = whole_rows([r.astype(half) for r in residuals])

    grad_res = [my_rows(cotangent, chunk).astype(single) for chunk in chunks]
    shares = [None] * depth
    for layer in reversed(range(depth)):
        gain_a, shift_a, gain_m, shift_m, bias_p, bias_s = [flat[layer, k] for k in range(6)]
        qkv, proj, expand, shrink = weights[layer]
        totals = None
        for which, chunk in enumerate(chunks):
            cosine, sine, allowed = masks[which]
            (normed, scaled, rows, rows_a, attn_in, mlp_in, queries, keys, values, attn_out, logsum, preact, activated) = saved[layer][which]
            grad_half = at.gather_rows(grad_res[which].astype(half))
            grad_half_a = at.attention_rows(grad_half)
            bias_grad = jnp.sum(grad_res[which], axis=0)
            slope = 0.5 * (1.0 + lax.erf(preact * root_half)) + preact * jnp.exp(-0.5 * preact * preact) * gauss_norm
            grad_preact = mm_t(grad_half, shrink) * slope
            unit_grad = jnp.sum(grad_preact, axis=0)
            grad_pre_half = grad_preact.astype(half)
            grad_mixed = mm_t(grad_half_a, proj).astype(half)
            gq, gk, gv = attend_back(queries, keys, values, allowed, logsum, grad_mixed)
            grad_proj = jnp.concatenate([rotate(gq, cosine, -sine), rotate(gk, cosine, -sine), gv], 1)
            head_grad = jnp.sum(grad_proj, axis=0)
            grad_proj_half = grad_proj.astype(half)
            grad_mlp_in = mm_t(grad_pre_half, expand)
            grad_attn_in = mm_t(grad_proj_half, qkv)
            weighted = at.add_attention_rows(grad_mlp_in * gain_m, grad_attn_in * gain_a)
            weighted = at.scatter_rows(weighted)
            rows32, rows_a32 = rows.astype(single), rows_a.astype(single)
            pieces = (
                t_mm(attn_in, grad_proj_half),
                t_mm(attn_out, grad_half_a),
                t_mm(mlp_in, grad_pre_half),
                t_mm(activated, grad_half),
                jnp.stack(
                    [
                        bias_grad,
                        jnp.sum(grad_attn_in * rows_a32, axis=0),
                        jnp.sum(grad_attn_in, axis=0),
                        jnp.sum(grad_mlp_in * rows32, axis=0),
                        jnp.sum(grad_mlp_in, axis=0),
                    ]
                ),
                unit_grad,
                head_grad,
            )
            totals = pieces if totals is None else tuple(a + b for a, b in zip(totals, pieces))
            grad_res[which] = grad_res[which] + scaled * (
                weighted
                - jnp.mean(weighted, axis=-1, keepdims=True)
                - normed * jnp.mean(weighted * normed, axis=-1, keepdims=True)
            )
        g_qkv, g_proj, g_expand, g_shrink, g_wide, g_units, g_head = totals
        g_qkv = at.scatter_head(g_qkv.reshape(at.n_dp, shard, 3 * head_width))
        g_qkv = g_qkv.reshape(heads_here, shard, 3, head_width).transpose(1, 2, 0, 3)
        g_proj = at.scatter_head(g_proj.reshape(head_width, at.n_dp, shard).transpose(1, 0, 2))
        g_expand = at.scatter_units(g_expand.reshape(at.n_a, 2, shard, units)).transpose(1, 0, 2)
        g_shrink = at.scatter_units(g_shrink.reshape(units, at.n_a, 2, shard).transpose(1, 2, 0, 3))
        g_wide = at.sum_over(g_wide.reshape(5 * at.n_dp, shard), "mp")
        g_units = put(jnp.zeros((at.n_a, units), single), g_units, at.a, 0).reshape(at.n_dp, shard)
        g_head = put(jnp.zeros((heads_here, 3, head_width), single), g_head.reshape(3, head_width), at.hi, 0)
        packed = jnp.concatenate(
            [g_wide, g_units, g_head.reshape(heads_here * 3, head_width).reshape(-1, shard)], 0
        )
        packed = at.sum_over(packed, "dp")
        g_wide = pick(packed[: 5 * at.n_dp].reshape(5, at.n_dp, shard), at.dp, 1)
        g_units = pick(packed[5 * at.n_dp : 6 * at.n_dp], at.dp, 0)
        g_head = packed[6 * at.n_dp :].reshape(heads_here, 3, at.n_dp, head_shard)
        g_head = pick(g_head, at.dp, 2).transpose(1, 0, 2)
        shares[layer] = (
            g_qkv.reshape(shard, 3, local_width),
            g_head,
            g_proj.reshape(local_width, shard),
            g_wide[0],
            g_expand.reshape(shard, -1),
            g_units[None],
            g_shrink.reshape(-1, shard),
            g_wide[0],
            g_wide[1],
            g_wide[2],
            g_wide[3],
            g_wide[4],
        )
    owned = tuple(jnp.stack([shares[layer][k] for layer in range(depth)]) for k in range(12))
    return (outputs, whole_rows(grad_res)) + owned


def solution(mesh):
    rows = P(None, "dp", None)
    specs = (
        P(None, "dp", None, "mp"),
        P(None, None, "mp", "dp"),
        P(None, "mp", "dp"),
        P(None, "dp"),
        P(None, "dp", "mp"),
        P(None, "mp", "dp"),
        P(None, "mp", "dp"),
        P(None, "dp"),
        P(None, "dp"),
        P(None, "dp"),
        P(None, "dp"),
        P(None, "dp"),
    )
    return jax.shard_map(
        on_device,
        mesh=mesh,
        in_specs=(rows, P(None, "dp"), rows) + specs,
        out_specs=(rows, rows) + specs,
        check_vma=False,
    )
```
